32 devices in a mesh: gx: 4 (over x, core), gy: 4 (over z), gz: 2 (over y).
Axes of the slice: x: 2, y: 2, z: 4, core: 2. Of those that a mesh axis runs over, the one named last changes fastest.
Arguments:
- fine_coef: bfloat16 [256, 512], P(('gx', 'gy', 'gz')), may hold values from -6 to 6
- mid_leaf: bfloat16 [32, 512], P(('gx', 'gy', 'gz')), may hold values from -6 to 6
- mid_child: int32 [32, 8], P(('gx', 'gy', 'gz')), may hold values from 0 to 7, as said below
- mid_parent: int32 [32], P(('gx', 'gy', 'gz')), may hold values from 0 to 31, each once
- mid_refined: int32 [32], P(('gx', 'gy', 'gz')), may hold values 0 or 1
- fine_nbr: int32 [256, 27], P(('gx', 'gy', 'gz')), may hold values from -1 to 255, as said below
- mid_nbr: int32 [32, 27], P(('gx', 'gy', 'gz')), may hold values from -1 to 31, as said below
- coarse_nbr: int32 [4, 27], replicated, may hold values from -1 to 3, as said below
- op_factor: float32 [3, 32, 3, 8, 8], replicated, may hold values from -1 to 1
- term_weight: float32 [32], replicated, may hold values from 0.05 to 1
Outputs:
- fine_out: float32 [256, 512], P(('gx', 'gy', 'gz'))
- mid_out: float32 [32, 512], P(('gx', 'gy', 'gz'))
The draws below stay inside these ranges and needn't reach their ends.
Inputs may be any that keep to these rules, and one draw needn't show every extreme that they name: `fine_nbr`: column d names the fine box adjacent across displacement (d // 9 - 1, d // 3 % 3 - 1, d % 3 - 1), or -1. Column 13 is the row's own box. Box g lies on device g // 8; the named box's device differs from the row's device along each of gx, gy, gz by 0 or by that component of the displacement. `mid_nbr`: column d names the middle box adjacent across displacement (d // 9 - 1, d // 3 % 3 - 1, d % 3 - 1), or -1. Column 13 is the row's own box. Box g lies on device g; the named box's device differs from the row's device along each of gx, gy, gz by 0 or by that component of the displacement. `coarse_nbr`: column d names the coarse box adjacent across displacement (d // 9 - 1, d // 3 % 3 - 1, d % 3 - 1), or -1. Column 13 is the row's own box. `mid_child`: the 1 row of one device together name each of its 8 local fine slots exactly once. `mid_parent`: each value appears once.
All inputs are finite; a program needn't handle non-finite values. No bound on the sum of `mid_refined` on one device may be relied on, other than what follows from the above.
Results may differ from the reference program's by a relative error of at most 0.006.
Values may be sent and summed in bfloat16 or wider, within the bound.
A program may use at most 64 MiB of HBM per device.

```python
import math
import jax
import jax.numpy as jnp
import numpy as np
from jax import lax

K = 8
TERMS = 32
MB_DEV = 1
FINE = 256
MID = 32
COARSE = 4
N_GX = 4
N_GY = 4
N_GZ = 2
DEVICES = 32


def near_boxes(key, per_device):
    box_total = per_device * DEVICES
    box_index = jnp.arange(box_total, dtype=jnp.int32)
    device = box_index // per_device
    coord_x = device // (N_GY * N_GZ)
    coord_y = device // N_GZ % N_GY
    coord_z = device % N_GZ
    column = jnp.arange(27, dtype=jnp.int32)
    step_x = column // 9 - 1
    step_y = column // 3 % 3 - 1
    step_z = column % 3 - 1
    key_hop, key_slot, key_gone = jax.random.split(key, 3)
    hop_bits = jax.random.randint(key_hop, (box_total, 3, 27), 0, 2, dtype=jnp.int32)
    near_x = coord_x[:, None] + step_x[None, :] * hop_bits[:, 0]
    near_y = coord_y[:, None] + step_y[None, :] * hop_bits[:, 1]
    near_z = coord_z[:, None] + step_z[None, :] * hop_bits[:, 2]
    inside = (near_x >= 0) & (near_x < N_GX) & (near_y >= 0) & (near_y < N_GY) & (near_z >= 0) & (near_z < N_GZ)
    slot_pick = jax.random.randint(key_slot, (box_total, 27), 0, per_device, dtype=jnp.int32)
    gone_mask = jax.random.randint(key_gone, (box_total, 27), 0, 5, dtype=jnp.int32) == 0
    named_box = ((near_x * N_GY + near_y) * N_GZ + near_z) * per_device + slot_pick
    result = jnp.where(inside & jnp.logical_not(gone_mask), named_box, -1)
    result = jnp.where(column[None, :] == 13, box_index[:, None], result)
    return result.astype(jnp.int32)


def draw_fine_nbr(key, part):
    return near_boxes(jax.random.fold_in(key, 11), 8 * MB_DEV)


def draw_mid_nbr(key, part):
    return near_boxes(jax.random.fold_in(key, 12), MB_DEV)


def draw_coarse_nbr(key, part):
    key_pick, key_gone = jax.random.split(jax.random.fold_in(key, 13), 2)
    column = jnp.arange(27, dtype=jnp.int32)
    box_index = jnp.arange(COARSE, dtype=jnp.int32)
    picked = jax.random.randint(key_pick, (COARSE, 27), 0, COARSE, dtype=jnp.int32)
    gone_mask = jax.random.randint(key_gone, (COARSE, 27), 0, 5, dtype=jnp.int32) == 0
    result = jnp.where(gone_mask, -1, picked)
    result = jnp.where(column[None, :] == 13, box_index[:, None], result)
    return result.astype(jnp.int32)


def shuffle_slots(single_key):
    return jax.random.permutation(single_key, 8 * MB_DEV)


def draw_mid_child(key, part):
    all_keys = jax.random.split(jax.random.fold_in(key, 14), DEVICES)
    orders = jax.vmap(shuffle_slots)(all_keys)
    return orders.reshape(MID, 8).astype(jnp.int32)


def place_ends(entries, key, low, top_value):
    index_at = [jax.random.randint(jax.random.fold_in(key, axis), (), 0, length) for axis, length in enumerate(entries.shape)]
    longest = entries.shape.index(max(entries.shape))
    next_to = index_at[:longest] + [(index_at[longest] + 1) % entries.shape[longest]] + index_at[longest + 1:]
    return entries.at[tuple(index_at)].set(low).at[tuple(next_to)].set(top_value)


def steps_of(rng, extent, shards, low, high):
    def one(axis_at, shards_of):
        draws = jax.random.uniform(jax.random.fold_in(jax.random.fold_in(rng, 6), axis_at), (shards_of,), jnp.float32, low / len(shards), high / len(shards))
        return jnp.repeat(jnp.exp(draws), extent[axis_at] // shards_of).reshape((-1,) + (1,) * (len(extent) - axis_at - 1))

    level = one(*shards[0])
    for cut in shards[1:]:
        level = level * one(*cut)
    return level


def normal_values(key, shape, scale, reach, cuts=(), held_as=jnp.bfloat16):
    array = jax.random.normal(key, shape, jnp.float32) * scale
    if len(cuts) > 0:
        array = steps_of(key, shape, cuts, -0.22, 0.18) * array
    return jnp.clip(array, min=-reach, max=reach).astype(held_as)


def setup_inputs(seed: int = 0) -> dict:
    keys = jax.random.split(jax.random.key(seed), 11)
    fine_coef = normal_values(keys[0], (FINE, K ** 3), 1.0, 6.0, ((0, 32),))
    mid_leaf = normal_values(keys[1], (MID, K ** 3), 1.0, 6.0, ((0, 32),))
    mid_child = draw_mid_child(jax.random.fold_in(keys[10], 71), 0)
    mid_parent = jax.random.permutation(keys[3], MID).astype(jnp.int32)
    mid_refined = place_ends((jax.random.randint(keys[4], (MID,), 0, 3) < 2).astype(jnp.int32), jax.random.fold_in(keys[4], 1), 0, 1)
    fine_nbr = draw_fine_nbr(jax.random.fold_in(keys[10], 71), 0)
    mid_nbr = draw_mid_nbr(jax.random.fold_in(keys[10], 71), 0)
    coarse_nbr = draw_coarse_nbr(jax.random.fold_in(keys[10], 71), 0)
    op_factor = normal_values(keys[8], (3, TERMS, 3, K, K), 0.16, 1.0, (), jnp.float32)
    term_weight = jnp.clip(jnp.exp(jax.random.uniform(keys[9], (TERMS,), jnp.float32, math.log(0.05), math.log(1.0))), 0.05, 1.0)
    return dict(fine_coef=fine_coef, mid_leaf=mid_leaf, mid_child=mid_child, mid_parent=mid_parent, mid_refined=mid_refined, fine_nbr=fine_nbr, mid_nbr=mid_nbr, coarse_nbr=coarse_nbr, op_factor=op_factor, term_weight=term_weight)


exact_mode = lax.Precision.HIGHEST

def poly_multiply(left, right):
    result = [0.0] * (len(left) + len(right) - 1)
    for first, left_coef in enumerate(left):
        for second, right_coef in enumerate(right):
            result[first + second] += left_coef * right_coef
    return result

def poly_compose(coeffs, factor, offset):
    result = [0.0]
    power_term = [1.0]
    for coef in coeffs:
        padded = result + [0.0] * (len(power_term) - len(result))
        result = [padded[place] + coef * power_term[place] for place in range(len(power_term))]
        power_term = poly_multiply(power_term, [offset, factor])
    return result

def legendre_table(basis_order):
    polys = [[1.0], [0.0, 1.0]]
    for degree in range(1, basis_order):
        upper = [0.0] + [(2 * degree + 1) * coef for coef in polys[degree]]
        lower = [degree * coef for coef in polys[degree - 1]] + [0.0] * (len(upper) - len(polys[degree - 1]))
        polys.append([(upper[place] - lower[place]) / (degree + 1) for place in range(len(upper))])
    return [[math.sqrt(2 * degree + 1) * coef for coef in poly_compose(polys[degree], 2.0, -1.0)] for degree in range(basis_order)]

def two_scale(basis_order):
    shifted = legendre_table(basis_order)
    filters = np.zeros((2, basis_order, basis_order))
    for which_half in range(2):
        for row_at in range(basis_order):
            halved = poly_compose(shifted[row_at], 0.5, 0.5 * which_half)
            for col_at in range(basis_order):
                product = poly_multiply(halved, shifted[col_at])
                total = sum((coef / (place + 1) for place, coef in enumerate(product)))
                filters[which_half, row_at, col_at] = total / math.sqrt(2.0)
    return jnp.asarray(filters, jnp.float32)

def compress(children, filters):
    box_count = children.shape[0]
    basis_order = filters.shape[1]
    cube_form = children.reshape(box_count, 2, 2, 2, basis_order, basis_order, basis_order)
    section_one = jnp.einsum('bijlxyz,ipx->bjlpyz', cube_form, filters, precision=exact_mode)
    section_two = jnp.einsum('bjlpyz,jqy->blpqz', section_one, filters, precision=exact_mode)
    section_three = jnp.einsum('blpqz,lrz->bpqr', section_two, filters, precision=exact_mode)
    return section_three.reshape(box_count, basis_order ** 3)

def prolong(parents, filters):
    box_count = parents.shape[0]
    basis_order = filters.shape[1]
    cube_form = parents.reshape(box_count, basis_order, basis_order, basis_order)
    section_one = jnp.einsum('bpqr,ipx->bixqr', cube_form, filters, precision=exact_mode)
    section_two = jnp.einsum('bixqr,jqy->bijxyr', section_one, filters, precision=exact_mode)
    section_three = jnp.einsum('bijxyr,lrz->bijlxyz', section_two, filters, precision=exact_mode)
    return section_three.reshape(box_count, 8, basis_order ** 3)

def level_tables(factors, weights):
    basis_order = factors.shape[-1]
    term_count = factors.shape[0]
    across = jnp.transpose(factors, (1, 0, 3, 2))
    blocks = weights[None, None, :, None, None, None, None] * across[:, None, :, :, None, :, None] * across[None, :, :, None, :, None, :]
    blocks = blocks.reshape(3, 3, term_count * basis_order * basis_order, basis_order * basis_order)
    return (factors.astype(jnp.bfloat16), blocks.astype(jnp.bfloat16))

def apply_boxes(sources, factor_bf, blocks):
    box_count = sources.shape[0]
    basis_order = factor_bf.shape[-1]
    plane_size = basis_order * basis_order
    cube_form = sources.reshape(box_count, 3, 3, 3, basis_order, plane_size)
    running = jnp.zeros((box_count * basis_order, plane_size), jnp.float32)
    for along_y in range(3):
        for along_z in range(3):
            picked = cube_form[:, :, along_y, along_z]
            mixed_terms = jnp.einsum('mdax,bdxq->bamq', factor_bf.astype(jnp.float32), picked.astype(jnp.float32), precision=exact_mode).astype(jnp.bfloat16)
            flat_terms = mixed_terms.reshape(box_count * basis_order, -1)
            running = running + jnp.dot(flat_terms.astype(jnp.float32), blocks[along_y, along_z].astype(jnp.float32), precision=exact_mode)
    return running.reshape(box_count, basis_order ** 3)

def apply_level(source_table, near_ids, factors, weights):
    factor_bf, blocks = level_tables(factors, weights)
    total_rows = near_ids.shape[0]
    block_rows = math.gcd(total_rows, 128)
    grouped = near_ids.reshape(total_rows // block_rows, block_rows, 27)

    def one_block(some_rows):
        sources = source_table[jnp.maximum(some_rows, 0)] * (some_rows >= 0)[:, :, None].astype(source_table.dtype)
        return apply_boxes(sources, factor_bf, blocks)
    return lax.map(one_block, grouped).reshape(total_rows, -1)

def reference(fine_coef, mid_leaf, mid_child, mid_parent, mid_refined, fine_nbr, mid_nbr, coarse_nbr, op_factor, term_weight):
    filters = two_scale(K)
    slots_dev = 8 * MB_DEV
    mid_count = mid_child.shape[0]
    volume = fine_coef.shape[1]
    owner_dev = jnp.arange(mid_count, dtype=jnp.int32) // MB_DEV
    child_rows = (owner_dev[:, None] * slots_dev + mid_child).astype(jnp.int32)
    flat_rows = child_rows.reshape(-1)
    refined = mid_refined.astype(jnp.float32)
    live_mask = jnp.zeros((FINE,), jnp.float32).at[flat_rows].set(jnp.repeat(refined, 8))
    children = fine_coef[child_rows].astype(jnp.float32)
    compressed = compress(children, filters)
    mid_source = jnp.where(mid_refined[:, None] > 0, compressed, mid_leaf.astype(jnp.float32)).astype(jnp.bfloat16)
    mid_float = mid_source.astype(jnp.float32)
    spread = prolong(mid_float, filters)
    fine_from = jnp.zeros((FINE, volume), jnp.float32).at[flat_rows].set(spread.reshape(-1, volume))
    fine_detail = (live_mask[:, None] * (fine_coef.astype(jnp.float32) - fine_from)).astype(jnp.bfloat16)
    parent = (mid_parent // 8).astype(jnp.int32)
    octant = mid_parent % 8
    octant_hot = (octant[:, None] == jnp.arange(8, dtype=jnp.int32)[None, :]).astype(jnp.float32)
    placed = octant_hot[:, :, None] * mid_float[:, None, :]
    coarse_source = jnp.zeros((COARSE, volume), jnp.float32).at[parent].add(compress(placed, filters))
    parent_source = coarse_source[parent]
    from_coarse = lax.optimization_barrier(jnp.sum(octant_hot[:, :, None] * prolong(parent_source, filters), axis=1))
    mid_detail = (mid_float - from_coarse).astype(jnp.bfloat16)
    coarse_table = coarse_source.astype(jnp.bfloat16)
    coarse_output = apply_level(coarse_table, coarse_nbr, op_factor[2], term_weight)
    parent_out = coarse_output[parent]
    mid_out = apply_level(mid_detail, mid_nbr, op_factor[1], term_weight) + lax.optimization_barrier(jnp.sum(octant_hot[:, :, None] * prolong(parent_out, filters), axis=1))
    fine_back = jnp.zeros((FINE, volume), jnp.float32).at[flat_rows].set(prolong(mid_out, filters).reshape(-1, volume))
    fine_out = live_mask[:, None] * (apply_level(fine_detail, fine_nbr, op_factor[0], term_weight) + fine_back)
    return (fine_out, mid_out)
```

```python
import math

import jax
import jax.numpy as jnp
import numpy as np
from jax import lax
from jax.experimental import pallas as pl
from jax.experimental.pallas import tpu as pltpu
from jax.sharding import PartitionSpec as P

exact_mode = lax.Precision.HIGHEST


def poly_multiply(left, right):
    result = [0.0] * (len(left) + len(right) - 1)
    for first, left_coef in enumerate(left):
        for second, right_coef in enumerate(right):
            result[first + second] += left_coef * right_coef
    return result


def poly_compose(coeffs, factor, offset):
    result = [0.0]
    power_term = [1.0]
    for coef in coeffs:
        padded = result + [0.0] * (len(power_term) - len(result))
        result = [padded[place] + coef * power_term[place] for place in range(len(power_term))]
        power_term = poly_multiply(power_term, [offset, factor])
    return result


def legendre_table(basis_order):
    polys = [[1.0], [0.0, 1.0]]
    for degree in range(1, basis_order):
        upper = [0.0] + [(2 * degree + 1) * coef for coef in polys[degree]]
        lower = [degree * coef for coef in polys[degree - 1]] + [0.0] * (
            len(upper) - len(polys[degree - 1])
        )
        polys.append([(upper[place] - lower[place]) / (degree + 1) for place in range(len(upper))])
    return [
        [math.sqrt(2 * degree + 1) * coef for coef in poly_compose(polys[degree], 2.0, -1.0)]
        for degree in range(basis_order)
    ]


def two_scale(basis_order):
    shifted = legendre_table(basis_order)
    filters = np.zeros((2, basis_order, basis_order))
    for which_half in range(2):
        for row_at in range(basis_order):
            halved = poly_compose(shifted[row_at], 0.5, 0.5 * which_half)
            for col_at in range(basis_order):
                product = poly_multiply(halved, shifted[col_at])
                total = sum((coef / (place + 1) for place, coef in enumerate(product)))
                filters[which_half, row_at, col_at] = total / math.sqrt(2.0)
    return jnp.asarray(filters, jnp.float32)


def compress(children, filters):
    box_count = children.shape[0]
    basis_order = filters.shape[1]
    cube_form = children.reshape(box_count, 2, 2, 2, basis_order, basis_order, basis_order)
    section_one = jnp.einsum("bijlxyz,ipx->bjlpyz", cube_form, filters, precision=exact_mode)
    section_two = jnp.einsum("bjlpyz,jqy->blpqz", section_one, filters, precision=exact_mode)
    section_three = jnp.einsum("blpqz,lrz->bpqr", section_two, filters, precision=exact_mode)
    return section_three.reshape(box_count, basis_order**3)


def prolong(parents, filters):
    box_count = parents.shape[0]
    basis_order = filters.shape[1]
    cube_form = parents.reshape(box_count, basis_order, basis_order, basis_order)
    section_one = jnp.einsum("bpqr,ipx->bixqr", cube_form, filters, precision=exact_mode)
    section_two = jnp.einsum("bixqr,jqy->bijxyr", section_one, filters, precision=exact_mode)
    section_three = jnp.einsum("bijxyr,lrz->bijlxyz", section_two, filters, precision=exact_mode)
    return section_three.reshape(box_count, 8, basis_order**3)


def local_rows(near_ids, per_device):
    size_y = lax.axis_size("gy")
    size_z = lax.axis_size("gz")
    mine_x = lax.axis_index("gx")
    mine_y = lax.axis_index("gy")
    mine_z = lax.axis_index("gz")
    device = near_ids // per_device
    slot_at = near_ids % per_device
    other_x = device // (size_y * size_z)
    other_y = device // size_z % size_y
    other_z = device % size_z
    cell_at = (other_x - mine_x + 1) * 9 + (other_y - mine_y + 1) * 3 + (other_z - mine_z + 1)
    return jnp.where(near_ids >= 0, cell_at * per_device + slot_at, -1)


MESH = pl.DeviceIdType.MESH
AXES = ("gx", "gy", "gz")
CHUNK = 4


def exchange_kernel(sizes, fine_ref, row_ref, halo, rows, own_sem, fs, fr, ms, mr):
    here = [lax.axis_index(axis) for axis in AXES]

    def peer(dim, offset):
        spot = list(here)
        spot[dim] = lax.rem(here[dim] + offset, sizes[dim])
        return tuple(spot)

    barrier = pltpu.get_barrier_semaphore()
    for dim in range(3):
        for offset in range(1, sizes[dim]):
            pl.semaphore_signal(barrier, inc=1, device_id=peer(dim, offset), device_id_type=MESH)
    own = [
        pltpu.make_async_copy(fine_ref, halo.at[1, 1, 1], own_sem.at[0]),
        pltpu.make_async_copy(row_ref, rows.at[here[0], here[1], here[2]], own_sem.at[1]),
    ]
    for copy in own:
        copy.start()
    for copy in own:
        copy.wait()
    pl.semaphore_wait(barrier, sum(sizes) - 3)
    views = (
        lambda k: halo.at[k],
        lambda k: halo.at[1, k],
        lambda k: halo.at[1, 1, k],
    )
    mine = (
        rows.at[here[0]],
        rows.at[here[0], here[1]],
        rows.at[here[0], here[1], here[2]],
    )
    for dim in (2, 1, 0):
        copies = []
        for side, (offset, land) in enumerate(((1, 0), (sizes[dim] - 1, 2))):
            copies.append(
                pltpu.make_async_remote_copy(
                    src_ref=views[dim](1),
                    dst_ref=views[dim](land),
                    send_sem=fs.at[dim, side],
                    recv_sem=fr.at[dim, side],
                    device_id=peer(dim, offset),
                    device_id_type=MESH,
                )
            )
        for offset in range(1, sizes[dim]):
            copies.append(
                pltpu.make_async_remote_copy(
                    src_ref=mine[dim],
                    dst_ref=mine[dim],
                    send_sem=ms.at[dim, offset],
                    recv_sem=mr.at[dim, offset],
                    device_id=peer(dim, offset),
                    device_id_type=MESH,
                )
            )
        for copy in copies:
            copy.start()
        for copy in copies:
            copy.wait()


def exchange(fine_detail, row):
    sizes = tuple(lax.axis_size(axis) for axis in AXES)
    most = max(sizes)
    vmem = pl.BlockSpec(memory_space=pltpu.VMEM)
    dma = pltpu.SemaphoreType.DMA
    return pl.pallas_call(
        lambda *refs: exchange_kernel(sizes, *refs),
        out_shape=(
            jax.ShapeDtypeStruct((3, 3, 3) + fine_detail.shape, fine_detail.dtype),
            jax.ShapeDtypeStruct(sizes + row.shape, row.dtype),
        ),
        in_specs=[vmem, vmem],
        out_specs=(vmem, vmem),
        scratch_shapes=[dma((2,)), dma((3, 2)), dma((3, 2)), dma((3, most)), dma((3, most))],
        compiler_params=pltpu.CompilerParams(collective_id=0, has_side_effects=True),
        name="exchange",
    )(fine_detail, row)


def apply_kernel(left_ref, right_ref, mix_ref, *refs):
    levels = mix_ref.shape[0]
    chunks, terms = left_ref.shape[1], mix_ref.shape[2]
    lanes = CHUNK * 64
    sources, outs, sums = refs[:levels], refs[levels : 2 * levels], refs[2 * levels :]
    pair = lax.broadcasted_iota(jnp.int32, (CHUNK * 8, lanes), 0)
    lane = lax.broadcasted_iota(jnp.int32, (CHUNK * 8, lanes), 1)
    same_term = pair // 8 == lane // 64
    outer = (same_term & (pair % 8 == lane // 8 % 8)).astype(jnp.float32)
    inner = (same_term & (pair % 8 == lane % 8)).astype(jnp.float32)
    term = lax.broadcasted_iota(jnp.int32, (terms, lanes), 0)
    term_lane = lax.broadcasted_iota(jnp.int32, (terms, lanes), 1) // 64
    for level in range(levels):
        total = sums[level]
        boxes = total.shape[1]
        total[...] = jnp.zeros_like(total)

        def step(c, carry, level=level, total=total, boxes=boxes):
            left = jnp.dot(left_ref[level, c], outer, precision=exact_mode,
                           preferred_element_type=jnp.float32)
            right = jnp.dot(right_ref[level, c], inner, precision=exact_mode,
                            preferred_element_type=jnp.float32)
            pick = (term == term_lane + c * CHUNK).astype(jnp.float32).astype(jnp.bfloat16)
            mix = jnp.dot(mix_ref[level], pick, preferred_element_type=jnp.float32)
            blocks = []
            for ey in range(3):
                for ez in range(3):
                    block = (left[ey * 8 : ey * 8 + 8][:, None, :]
                             * right[ez * 8 : ez * 8 + 8][None, :, :])
                    blocks.append(block.reshape(64, lanes).astype(jnp.bfloat16))
            table = jnp.concatenate(blocks, axis=0)
            spread = jnp.dot(sources[level][...], table, preferred_element_type=jnp.float32)
            spread = spread.reshape(boxes, 3, 8, lanes)
            for a in range(8):
                factor = mix[a * 24 : a * 24 + 24].reshape(3, 8, lanes)
                total[a] += jnp.sum(spread * factor[None], axis=1)
            return carry

        lax.fori_loop(0, chunks, step, 0)
        for a in range(8):
            folded = jnp.sum(total[a], axis=1)
            result = folded[:, :64]
            for k in range(1, CHUNK):
                result = result + folded[:, k * 64 : k * 64 + 64]
            outs[level][a] = result


def apply_levels(factors, weights, sources):
    levels, terms = factors.shape[:2]
    chunks = terms // CHUNK
    right = jnp.transpose(
        factors.reshape(levels, chunks, CHUNK, 3, 8, 8), (0, 1, 3, 5, 2, 4)
    )
    left = right * weights.reshape(1, chunks, 1, 1, CHUNK, 1)
    right = right.reshape(levels, chunks, 24, CHUNK * 8)
    left = left.reshape(levels, chunks, 24, CHUNK * 8)
    mix = jnp.transpose(factors.astype(jnp.bfloat16), (0, 3, 2, 4, 1)).reshape(
        levels, 192, terms
    )
    counts = [source.shape[0] // 24 for source in sources]
    vmem = pl.BlockSpec(memory_space=pltpu.VMEM)
    outs = pl.pallas_call(
        apply_kernel,
        out_shape=tuple(jax.ShapeDtypeStruct((8, n, 64), jnp.float32) for n in counts),
        in_specs=[vmem] * (3 + levels),
        out_specs=tuple(vmem for _ in counts),
        scratch_shapes=[pltpu.VMEM((8, n, 8, CHUNK * 64), jnp.float32) for n in counts],
        name="apply_levels",
    )(left, right, mix, *sources)
    return [
        jnp.transpose(out, (1, 0, 2)).reshape(n, 512) for out, n in zip(outs, counts)
    ]


def pick_sources(table, ids):
    boxes = ids.shape[0]
    picked = table[jnp.maximum(ids, 0)] * (ids >= 0)[:, :, None].astype(jnp.bfloat16)
    picked = picked.reshape(boxes, 3, 9, 8, 64)
    return jnp.transpose(picked, (0, 1, 3, 2, 4)).reshape(boxes * 24, 576)


def shards(
    fine_coef,
    mid_leaf,
    mid_child,
    mid_parent,
    mid_refined,
    fine_nbr,
    mid_nbr,
    coarse_nbr,
    op_factor,
    term_weight,
):
    basis_order = op_factor.shape[-1]
    filters = two_scale(basis_order)
    mid_local = mid_child.shape[0]
    slots_dev = fine_coef.shape[0]
    coarse_count = coarse_nbr.shape[0]
    child_hot = (
        mid_child[:, :, None] == jnp.arange(slots_dev, dtype=jnp.int32)[None, None, :]
    ).astype(jnp.float32)
    refined = mid_refined.astype(jnp.float32)
    live_mask = jnp.sum(child_hot * refined[:, None, None], axis=(0, 1))
    children = fine_coef[mid_child].astype(jnp.float32)
    compressed = compress(children, filters)
    mid_source = jnp.where(
        mid_refined[:, None] > 0, compressed, mid_leaf.astype(jnp.float32)
    ).astype(jnp.bfloat16)
    mid_float = mid_source.astype(jnp.float32)
    spread = prolong(mid_float, filters)
    fine_from = jnp.einsum("mos,mok->sk", child_hot, spread, precision=exact_mode)
    fine_detail = (live_mask[:, None] * (fine_coef.astype(jnp.float32) - fine_from)).astype(
        jnp.bfloat16
    )
    parent = mid_parent // 8
    octant = mid_parent % 8
    place = jnp.stack([parent, octant], axis=1).astype(jnp.bfloat16)
    row = jnp.concatenate(
        [mid_source, jnp.pad(place, ((0, 0), (0, 510)))], axis=1
    ).reshape(mid_local, 8, 128)
    halo, rows = exchange(fine_detail, row)
    rows = rows.reshape(-1, 1024)
    mid_all = rows[:, :512]
    place_all = rows[:, 512:514].astype(jnp.int32)
    parent_all = place_all[:, 0] * 8 + place_all[:, 1]
    slot_hot = (
        jnp.arange(coarse_count * 8, dtype=jnp.int32)[:, None] == parent_all[None, :]
    ).astype(jnp.bfloat16)
    slots = jnp.dot(slot_hot, mid_all, preferred_element_type=jnp.float32)
    coarse_source = compress(slots.reshape(coarse_count, 8, 512), filters)
    from_coarse = prolong(coarse_source, filters).reshape(coarse_count * 8, 512)
    mid_table = (slots - from_coarse).astype(jnp.bfloat16)
    coarse_table = coarse_source.astype(jnp.bfloat16)
    fine_picked = pick_sources(halo.reshape(-1, 512), local_rows(fine_nbr, slots_dev))
    near_slot = jnp.where(mid_nbr >= 0, parent_all[jnp.maximum(mid_nbr, 0)], -1)
    mid_picked = pick_sources(mid_table, near_slot)
    coarse_picked = pick_sources(coarse_table, coarse_nbr[parent])
    fine_direct, mid_direct, parent_out = apply_levels(
        op_factor, term_weight, [fine_picked, mid_picked, coarse_picked]
    )
    octant_hot = (octant[:, None] == jnp.arange(8, dtype=jnp.int32)[None, :]).astype(jnp.float32)
    mid_out = mid_direct + jnp.sum(
        octant_hot[:, :, None] * prolong(parent_out, filters), axis=1
    )
    fine_back = jnp.einsum(
        "mos,mok->sk", child_hot, prolong(mid_out, filters), precision=exact_mode
    )
    fine_out = live_mask[:, None] * (fine_direct + fine_back)
    return (fine_out, mid_out)


def solution(mesh):
    return jax.shard_map(
        shards,
        mesh=mesh,
        in_specs=(
            P(("gx", "gy", "gz"), None),
            P(("gx", "gy", "gz"), None),
            P(("gx", "gy", "gz"), None),
            P(("gx", "gy", "gz")),
            P(("gx", "gy", "gz")),
            P(("gx", "gy", "gz"), None),
            P(("gx", "gy", "gz"), None),
            P(),
            P(),
            P(),
        ),
        out_specs=(P(("gx", "gy", "gz"), None), P(("gx", "gy", "gz"), None)),
        check_vma=False,
    )
```

```python
import math

import jax
import jax.numpy as jnp
import numpy as np
from jax import lax
from jax.experimental import pallas as pl
from jax.experimental.pallas import tpu as pltpu
from jax.sharding import PartitionSpec as P

exact_mode = lax.Precision.HIGHEST


def poly_multiply(left, right):
    result = [0.0] * (len(left) + len(right) - 1)
    for first, left_coef in enumerate(left):
        for second, right_coef in enumerate(right):
            result[first + second] += left_coef * right_coef
    return result


def poly_compose(coeffs, factor, offset):
    result = [0.0]
    power_term = [1.0]
    for coef in coeffs:
        padded = result + [0.0] * (len(power_term) - len(result))
        result = [padded[place] + coef * power_term[place] for place in range(len(power_term))]
        power_term = poly_multiply(power_term, [offset, factor])
    return result


def legendre_table(basis_order):
    polys = [[1.0], [0.0, 1.0]]
    for degree in range(1, basis_order):
        upper = [0.0] + [(2 * degree + 1) * coef for coef in polys[degree]]
        lower = [degree * coef for coef in polys[degree - 1]] + [0.0] * (
            len(upper) - len(polys[degree - 1])
        )
        polys.append([(upper[place] - lower[place]) / (degree + 1) for place in range(len(upper))])
    return [
        [math.sqrt(2 * degree + 1) * coef for coef in poly_compose(polys[degree], 2.0, -1.0)]
        for degree in range(basis_order)
    ]


def two_scale(basis_order):
    shifted = legendre_table(basis_order)
    filters = np.zeros((2, basis_order, basis_order))
    for which_half in range(2):
        for row_at in range(basis_order):
            halved = poly_compose(shifted[row_at], 0.5, 0.5 * which_half)
            for col_at in range(basis_order):
                product = poly_multiply(halved, shifted[col_at])
                total = sum((coef / (place + 1) for place, coef in enumerate(product)))
                filters[which_half, row_at, col_at] = total / math.sqrt(2.0)
    return np.asarray(filters, np.float32)


def compress(children, filters):
    box_count = children.shape[0]
    basis_order = filters.shape[1]
    cube_form = children.reshape(box_count, 2, 2, 2, basis_order, basis_order, basis_order)
    section_one = jnp.einsum("bijlxyz,ipx->bjlpyz", cube_form, filters, precision=exact_mode)
    section_two = jnp.einsum("bjlpyz,jqy->blpqz", section_one, filters, precision=exact_mode)
    section_three = jnp.einsum("blpqz,lrz->bpqr", section_two, filters, precision=exact_mode)
    return section_three.reshape(box_count, basis_order**3)


def prolong(parents, filters):
    box_count = parents.shape[0]
    basis_order = filters.shape[1]
    cube_form = parents.reshape(box_count, basis_order, basis_order, basis_order)
    section_one = jnp.einsum("bpqr,ipx->bixqr", cube_form, filters, precision=exact_mode)
    section_two = jnp.einsum("bixqr,jqy->bijxyr", section_one, filters, precision=exact_mode)
    section_three = jnp.einsum("bijxyr,lrz->bijlxyz", section_two, filters, precision=exact_mode)
    return section_three.reshape(box_count, 8, basis_order**3)


def local_rows(near_ids, per_device):
    size_y = lax.axis_size("gy")
    size_z = lax.axis_size("gz")
    mine_x = lax.axis_index("gx")
    mine_y = lax.axis_index("gy")
    mine_z = lax.axis_index("gz")
    device = near_ids // per_device
    slot_at = near_ids % per_device
    other_x = device // (size_y * size_z)
    other_y = device // size_z % size_y
    other_z = device % size_z
    cell_at = (other_x - mine_x + 1) * 9 + (other_y - mine_y + 1) * 3 + (other_z - mine_z + 1)
    return jnp.where(near_ids >= 0, cell_at * per_device + slot_at, -1)


MESH = pl.DeviceIdType.MESH
AXES = ("gx", "gy", "gz")
CHUNK = 4


def exchange_kernel(sizes, fine_ref, row_ref, halo, rows, own_sem, fs, fr, ms, mr):
    here = [lax.axis_index(axis) for axis in AXES]

    def peer(dim, offset):
        spot = list(here)
        spot[dim] = lax.rem(here[dim] + offset, sizes[dim])
        return tuple(spot)

    barrier = pltpu.get_barrier_semaphore()
    for dim in range(3):
        for offset in range(1, sizes[dim]):
            pl.semaphore_signal(barrier, inc=1, device_id=peer(dim, offset), device_id_type=MESH)
    own = [
        pltpu.make_async_copy(fine_ref, halo.at[1, 1, 1], own_sem.at[0]),
        pltpu.make_async_copy(row_ref, rows.at[here[0], here[1], here[2]], own_sem.at[1]),
    ]
    for copy in own:
        copy.start()
    for copy in own:
        copy.wait()
    pl.semaphore_wait(barrier, sum(sizes) - 3)
    views = (
        lambda k: halo.at[k],
        lambda k: halo.at[1, k],
        lambda k: halo.at[1, 1, k],
    )
    mine = (
        rows.at[here[0]],
        rows.at[here[0], here[1]],
        rows.at[here[0], here[1], here[2]],
    )
    for dim in (2, 1, 0):
        copies = []
        for side, (offset, land) in enumerate(((1, 0), (sizes[dim] - 1, 2))):
            copies.append(
                pltpu.make_async_remote_copy(
                    src_ref=views[dim](1),
                    dst_ref=views[dim](land),
                    send_sem=fs.at[dim, side],
                    recv_sem=fr.at[dim, side],
                    device_id=peer(dim, offset),
                    device_id_type=MESH,
                )
            )
        for offset in range(1, sizes[dim]):
            copies.append(
                pltpu.make_async_remote_copy(
                    src_ref=mine[dim],
                    dst_ref=mine[dim],
                    send_sem=ms.at[dim, offset],
                    recv_sem=mr.at[dim, offset],
                    device_id=peer(dim, offset),
                    device_id_type=MESH,
                )
            )
        for copy in copies:
            copy.start()
        for copy in copies:
            copy.wait()


def exchange(fine_detail, row):
    sizes = tuple(lax.axis_size(axis) for axis in AXES)
    most = max(sizes)
    vmem = pl.BlockSpec(memory_space=pltpu.VMEM)
    dma = pltpu.SemaphoreType.DMA
    return pl.pallas_call(
        lambda *refs: exchange_kernel(sizes, *refs),
        out_shape=(
            jax.ShapeDtypeStruct((3, 3, 3) + fine_detail.shape, fine_detail.dtype),
            jax.ShapeDtypeStruct(sizes + row.shape, row.dtype),
        ),
        in_specs=[vmem, vmem],
        out_specs=(vmem, vmem),
        scratch_shapes=[dma((2,)), dma((3, 2)), dma((3, 2)), dma((3, most)), dma((3, most))],
        compiler_params=pltpu.CompilerParams(collective_id=0, has_side_effects=True),
        name="exchange",
    )(fine_detail, row)


def apply_kernel(right_ref, weight_ref, mix_ref, wide_ref, tall_ref, live_ref, child_ref, octant_ref, *refs):
    levels = mix_ref.shape[0]
    chunks, terms = right_ref.shape[1], mix_ref.shape[2]
    lanes = CHUNK * 64
    sources, (fine_ref, mid_ref), sums = refs[:levels], refs[levels : levels + 2], refs[levels + 2 :]
    applied = []
    pair = lax.broadcasted_iota(jnp.int32, (CHUNK * 8, lanes), 0)
    lane = lax.broadcasted_iota(jnp.int32, (CHUNK * 8, lanes), 1)
    same_term = pair // 8 == lane // 64
    outer = (same_term & (pair % 8 == lane // 8 % 8)).astype(jnp.float32)
    inner = (same_term & (pair % 8 == lane % 8)).astype(jnp.float32)
    term = lax.broadcasted_iota(jnp.int32, (terms, lanes), 0)
    term_lane = lax.broadcasted_iota(jnp.int32, (terms, lanes), 1) // 64
    for level in range(levels):
        total = sums[level]
        boxes = total.shape[1]
        total[...] = jnp.zeros_like(total)

        def step(c, carry, level=level, total=total, boxes=boxes):
            left = jnp.dot(right_ref[level, c] * weight_ref[c], outer, precision=exact_mode,
                           preferred_element_type=jnp.float32)
            right = jnp.dot(right_ref[level, c], inner, precision=exact_mode,
                            preferred_element_type=jnp.float32)
            pick = (term == term_lane + c * CHUNK).astype(jnp.float32).astype(jnp.bfloat16)
            mix = jnp.dot(mix_ref[level], pick, preferred_element_type=jnp.float32)
            blocks = []
            for ey in range(3):
                for ez in range(3):
                    block = (left[ey * 8 : ey * 8 + 8][:, None, :]
                             * right[ez * 8 : ez * 8 + 8][None, :, :])
                    blocks.append(block.reshape(64, lanes).astype(jnp.bfloat16))
            table = jnp.concatenate(blocks, axis=0)
            spread = jnp.dot(sources[level][...], table, preferred_element_type=jnp.float32)
            spread = spread.reshape(boxes, 3, 8, lanes)
            for a in range(8):
                factor = mix[a * 24 : a * 24 + 24].reshape(3, 8, lanes)
                total[a] += jnp.sum(spread * factor[None], axis=1)
            return carry

        lax.fori_loop(0, chunks, step, 0)
        planes = []
        for a in range(8):
            folded = jnp.sum(total[a], axis=1)
            result = folded[:, :64]
            for k in range(1, CHUNK):
                result = result + folded[:, k * 64 : k * 64 + 64]
            planes.append(result)
        applied.append(jnp.stack(planes, axis=1))

    def children(block):
        wide = jnp.dot(block, wide_ref[...], precision=exact_mode,
                       preferred_element_type=jnp.float32)
        tall = jnp.dot(tall_ref[...], wide, precision=exact_mode,
                       preferred_element_type=jnp.float32)
        return [
            tall[o // 4 * 8 : o // 4 * 8 + 8, o % 4 * 64 : o % 4 * 64 + 64] for o in range(8)
        ]

    fine_direct, mid_direct, parent_out = applied
    slots, mids = fine_direct.shape[0], mid_direct.shape[0]
    totals = [fine_direct[slot] for slot in range(slots)]
    for m in range(mids):
        mid_out = mid_direct[m]
        for o, block in enumerate(children(parent_out[m])):
            mid_out = mid_out + octant_ref[m, o] * block
        mid_ref[m] = mid_out
        for o, block in enumerate(children(mid_out)):
            for slot in range(slots):
                totals[slot] = totals[slot] + child_ref[m * 8 + o, slot] * block
    for slot in range(slots):
        fine_ref[slot] = live_ref[0, slot] * totals[slot]


def apply_levels(factors, weights, sources, live_mask, child_hot, octant_hot, filters):
    levels, terms = factors.shape[:2]
    chunks = terms // CHUNK
    right = jnp.transpose(
        factors.reshape(levels, chunks, CHUNK, 3, 8, 8), (0, 1, 3, 5, 2, 4)
    ).reshape(levels, chunks, 24, CHUNK * 8)
    weight_rows = jnp.repeat(weights, 8).reshape(chunks, 1, CHUNK * 8)
    mix = jnp.transpose(factors.astype(jnp.bfloat16), (0, 3, 2, 4, 1)).reshape(
        levels, 192, terms
    )
    wide = np.einsum("jqy,lrz->qrjlyz", filters, filters).reshape(64, 256)
    tall = np.einsum("ipx->ixp", filters).reshape(16, 8)
    counts = [source.shape[0] // 24 for source in sources]
    vmem = pl.BlockSpec(memory_space=pltpu.VMEM)
    smem = pl.BlockSpec(memory_space=pltpu.SMEM)
    outs = pl.pallas_call(
        apply_kernel,
        out_shape=tuple(jax.ShapeDtypeStruct((n, 8, 64), jnp.float32) for n in counts[:2]),
        in_specs=[vmem] * 5 + [smem] * 3 + [vmem] * levels,
        out_specs=(vmem, vmem),
        scratch_shapes=[pltpu.VMEM((8, n, 8, CHUNK * 64), jnp.float32) for n in counts],
        name="apply_levels",
    )(
        right,
        weight_rows,
        mix,
        jnp.asarray(wide),
        jnp.asarray(tall),
        live_mask[None, :],
        child_hot.reshape(-1, child_hot.shape[-1]),
        octant_hot,
        *sources,
    )
    return tuple(out.reshape(-1, 512) for out in outs)


def pick_sources(table, ids):
    boxes = ids.shape[0]
    picked = table[jnp.maximum(ids, 0)] * (ids >= 0)[:, :, None].astype(jnp.bfloat16)
    picked = picked.reshape(boxes, 3, 9, 8, 64)
    return jnp.transpose(picked, (0, 1, 3, 2, 4)).reshape(boxes * 24, 576)


def shards(
    fine_coef,
    mid_leaf,
    mid_child,
    mid_parent,
    mid_refined,
    fine_nbr,
    mid_nbr,
    coarse_nbr,
    op_factor,
    term_weight,
):
    basis_order = op_factor.shape[-1]
    filters = two_scale(basis_order)
    mid_local = mid_child.shape[0]
    slots_dev = fine_coef.shape[0]
    coarse_count = coarse_nbr.shape[0]
    child_hot = (
        mid_child[:, :, None] == jnp.arange(slots_dev, dtype=jnp.int32)[None, None, :]
    ).astype(jnp.float32)
    refined = mid_refined.astype(jnp.float32)
    live_mask = jnp.sum(child_hot * refined[:, None, None], axis=(0, 1))
    children = fine_coef[mid_child].astype(jnp.float32)
    compressed = compress(children, filters)
    mid_source = jnp.where(
        mid_refined[:, None] > 0, compressed, mid_leaf.astype(jnp.float32)
    ).astype(jnp.bfloat16)
    mid_float = mid_source.astype(jnp.float32)
    spread = prolong(mid_float, filters)
    fine_from = jnp.einsum("mos,mok->sk", child_hot, spread, precision=exact_mode)
    fine_detail = (live_mask[:, None] * (fine_coef.astype(jnp.float32) - fine_from)).astype(
        jnp.bfloat16
    )
    parent = mid_parent // 8
    octant = mid_parent % 8
    place = jnp.stack([parent, octant], axis=1).astype(jnp.bfloat16)
    row = jnp.concatenate(
        [mid_source, jnp.pad(place, ((0, 0), (0, 510)))], axis=1
    ).reshape(mid_local, 8, 128)
    halo, rows = exchange(fine_detail, row)
    rows = rows.reshape(-1, 1024)
    mid_all = rows[:, :512]
    place_all = rows[:, 512:514].astype(jnp.int32)
    parent_all = place_all[:, 0] * 8 + place_all[:, 1]
    slot_hot = (
        jnp.arange(coarse_count * 8, dtype=jnp.int32)[:, None] == parent_all[None, :]
    ).astype(jnp.bfloat16)
    slots = jnp.dot(slot_hot, mid_all, preferred_element_type=jnp.float32)
    coarse_source = compress(slots.reshape(coarse_count, 8, 512), filters)
    from_coarse = prolong(coarse_source, filters).reshape(coarse_count * 8, 512)
    mid_table = (slots - from_coarse).astype(jnp.bfloat16)
    coarse_table = coarse_source.astype(jnp.bfloat16)
    fine_picked = pick_sources(halo.reshape(-1, 512), local_rows(fine_nbr, slots_dev))
    near_slot = jnp.where(mid_nbr >= 0, parent_all[jnp.maximum(mid_nbr, 0)], -1)
    mid_picked = pick_sources(mid_table, near_slot)
    coarse_picked = pick_sources(coarse_table, coarse_nbr[parent])
    octant_hot = (octant[:, None] == jnp.arange(8, dtype=jnp.int32)[None, :]).astype(jnp.float32)
    return apply_levels(
        op_factor,
        term_weight,
        [fine_picked, mid_picked, coarse_picked],
        live_mask,
        child_hot,
        octant_hot,
        filters,
    )


def solution(mesh):
    return jax.shard_map(
        shards,
        mesh=mesh,
        in_specs=(
            P(("gx", "gy", "gz"), None),
            P(("gx", "gy", "gz"), None),
            P(("gx", "gy", "gz"), None),
            P(("gx", "gy", "gz")),
            P(("gx", "gy", "gz")),
            P(("gx", "gy", "gz"), None),
            P(("gx", "gy", "gz"), None),
            P(),
            P(),
            P(),
        ),
        out_specs=(P(("gx", "gy", "gz"), None), P(("gx", "gy", "gz"), None)),
        check_vma=False,
    )
```
